32 devices in a mesh: group: 4 (over z), expert: 4 (over y, x), replica: 2 (over core).
Axes of the slice: x: 2, y: 2, z: 4, core: 2. Of those that a mesh axis runs over, the one named last changes fastest.
Arguments:
- cotangent: bfloat16 [1024, 2048], P(('group', 'expert')), may hold values from -6 to 6
- expert_ids: int32 [2, 1024, 4], P('replica', ('group', 'expert')), may hold values from 0 to 7, all different within a row; in each aligned block of 64 rows (0 to 63, 64 to 127, ..., all dimensions but the last counted through in order) at most 64 rows name the same one
- gate_probs: float32 [2, 1024, 4], P('replica', ('group', 'expert')), may hold values from 0.05 to 1
- saved_gate: bfloat16 [16, 2048, 384], P(('group', 'expert'), 'replica'), may hold values from -6 to 6
- saved_up: bfloat16 [16, 2048, 384], P(('group', 'expert'), 'replica'), may hold values from -6 to 6
- w_gate: bfloat16 [16, 2048, 384], P(('group', 'expert')), may hold values from -0.21875 to 0.21875
- w_up: bfloat16 [16, 2048, 384], P(('group', 'expert')), may hold values from -0.21875 to 0.21875
- w_down: bfloat16 [16, 384, 2048], P(('group', 'expert')), may hold values from -0.21875 to 0.21875
Outputs:
- grad_input: bfloat16 [1024, 2048], P(('group', 'expert'), 'replica')
- grad_down: float32 [16, 384, 2048], P(('group', 'expert'), None, 'replica')
The draws below stay inside these ranges and needn't reach their ends.
Inputs may be any that keep to these rules, and one draw needn't show every extreme that they name: `expert_ids`: each row of 4 entries names different experts. For each replica index and each block of 64 tokens no expert is named more than 64 times, and in every draw some expert is named exactly 64 times in some block.
All inputs are finite; a program needn't handle non-finite values.
Results may differ from the reference program's by a relative error of at most 0.0071.
Values may be sent and summed in bfloat16 or wider, within the bound.
A program may use at most 64 MiB of HBM per device.

```python
import math
import jax
import jax.numpy as jnp
import numpy as np
from jax import lax

D = 2048
FF = 768
TOK_DEV = 64
KREP = 4
EXPERTS = 8
UNITS = 16
FFH = 384
CAP = 64
SLOTS = 1024
TOKENS = 1024
N_GROUP = 4
N_EXPERT = 4
N_REPLICA = 2


def level_of(key, shape, pieces, low, largest):
    def one(position, shards_of):
        draws = jax.random.uniform(jax.random.fold_in(jax.random.fold_in(key, 6), position), (shards_of,), jnp.float32, low / len(pieces), largest / len(pieces))
        return jnp.repeat(jnp.exp(draws), shape[position] // shards_of).reshape((-1,) + (1,) * (len(shape) - position - 1))

    gain = one(*pieces[0])
    for cut in pieces[1:]:
        gain = gain * one(*cut)
    return gain


def shared_out(key, own, number, rows, number_of, top, limit, skew):
    order = jax.random.permutation(key, number_of)
    heavy_load, usual = load_shares(number_of, rows * top, limit, skew, True), load_shares(number_of, rows * top, limit, skew, False)
    places = jnp.arange(number_of)

    def named(lengths, rotation):
        used = int((lengths > 0).sum())
        fixed = max(1, used // 4)
        passed = fixed + (places - fixed + rotation * (used - fixed)) % max(1, number_of - fixed)
        return jnp.zeros((number_of,), jnp.int32).at[order[jnp.where(places < fixed, places, passed)]].set(jnp.asarray(lengths, jnp.int32))

    lengths = jnp.where(number % 4 == 0, named(heavy_load, number // 4), named(usual, number - number // 4 - 1))
    mixed = jax.random.permutation(jax.random.fold_in(own, 3), number_of)
    giver, sink = mixed[0:number_of // 2 * 2:2], mixed[1:number_of // 2 * 2:2]
    margin = jnp.minimum(lengths[giver] - 1, limit - lengths[sink]) // 2
    margin = jnp.where((giver == order[0]) | (sink == order[0]) | (lengths[sink] == 0), 0, jnp.maximum(margin, 0))
    passed = jax.random.randint(jax.random.fold_in(own, 4), (number_of // 2,), 0, 1 << 20) % (margin + 1)
    lengths = lengths.at[giver].add(-passed).at[sink].add(passed)
    items = jnp.searchsorted(jnp.cumsum(lengths), jnp.arange(rows * top), side="right").astype(jnp.int32)
    listing = items.reshape(top, rows).T
    listing = listing[jax.random.permutation(jax.random.fold_in(own, 1), rows)]
    rotation = jax.random.randint(jax.random.fold_in(own, 2), (rows, 1), 0, top)
    return jnp.take_along_axis(listing, (jnp.arange(top)[None, :] + rotation) % top, axis=1)


def load_shares(amount, total, most, lean, full):
    weights = [(1 << 20) // math.isqrt(standing ** lean) + 1 for standing in range(1, amount + 1)]
    largest = most if full else min(most, max(-(-total // amount), total * weights[0] // sum(weights)))
    least = 1 if total - largest >= amount - 1 else 0
    counts, spare = [largest] + [least] * (amount - 1), total - largest - least * (amount - 1)
    while spare > 0:
        candidates = [i for i in range(1, amount) if counts[i] < largest] or [i for i in range(1, amount) if counts[i] < most]
        whole, budget = sum([weights[i] for i in candidates]), spare
        for i in candidates:
            addition = min(most - counts[i], max(1, budget * weights[i] // whole), spare)
            counts[i] = counts[i] + addition
            spare = spare - addition
    return np.array(counts)


def scatter_about(key, dims, width, bound, shards=(), kind=jnp.bfloat16):
    drawn = jax.random.normal(key, dims, jnp.float32) * width
    if len(shards) > 0:
        drawn = level_of(key, dims, shards, -0.22, 0.18) * drawn
    return jnp.clip(drawn, min=-bound, max=bound).astype(kind)


def setup_inputs(seed: int = 0) -> dict:
    splits = jax.random.split(jax.random.key(seed), 9)
    cotangent = scatter_about(splits[0], (TOKENS, D), 1.0, 6.0, ((0, 16),))
    expert_ids_keys = jax.random.split(jax.random.fold_in(splits[1], 1), N_REPLICA * TOKENS // TOK_DEV)
    expert_ids_turns = jax.random.permutation(jax.random.fold_in(splits[1], 3), N_REPLICA * TOKENS // TOK_DEV)
    expert_ids = jax.vmap(lambda own, number: shared_out(jax.random.fold_in(splits[1], 2), own, number, TOK_DEV, EXPERTS, KREP, CAP, 2))(expert_ids_keys, expert_ids_turns).reshape((N_REPLICA, TOKENS, KREP))
    gate_probs = jnp.clip(jnp.exp(math.log(1.0) - 2.9957323 * jax.random.uniform(splits[2], (N_REPLICA, TOKENS, KREP), jnp.float32) ** level_of(splits[2], (N_REPLICA, TOKENS, KREP), ((0, 2), (1, 16)), -0.2, 0.2)), 0.05, 1.0)
    saved_gate = scatter_about(splits[3], (UNITS, N_REPLICA * SLOTS, FFH), 1.0, 6.0, ((0, 16), (1, 2)))
    saved_up = scatter_about(splits[4], (UNITS, N_REPLICA * SLOTS, FFH), 1.0, 6.0, ((0, 16), (1, 2)))
    w_gate = scatter_about(splits[5], (UNITS, D, FFH), FF ** -0.5, 0.21875, ((0, 16),))
    w_up = scatter_about(splits[6], (UNITS, D, FFH), FF ** -0.5, 0.21875, ((0, 16),))
    w_down = scatter_about(splits[7], (UNITS, FFH, D), FF ** -0.5, 0.21875, ((0, 16),))
    return {"cotangent": cotangent, "expert_ids": expert_ids, "gate_probs": gate_probs, "saved_gate": saved_gate, "saved_up": saved_up, "w_gate": w_gate, "w_up": w_up, "w_down": w_down}


def slots_of(id_row):
    positions = jnp.arange(id_row.shape[0], dtype=jnp.int32)
    same_expert = (id_row[:, None] == id_row[None, :]) & (positions[None, :] < positions[:, None])
    return jnp.sum(same_expert.astype(jnp.int32), axis=1)


def reference(cotangent, expert_ids, gate_probs, saved_gate, saved_up, w_gate, w_up, w_down):
    ndev = N_GROUP * N_EXPERT
    blocks = N_REPLICA * ndev
    assigned = TOK_DEV * KREP
    flat_ids = expert_ids.reshape(blocks, assigned).astype(jnp.int32)
    slot_pos = jax.vmap(slots_of)(flat_ids)
    scaled = (gate_probs[:, :, :, None] * cotangent[None, :, None, :].astype(jnp.float32)).astype(jnp.bfloat16)
    scaled = scaled.reshape(blocks, assigned, D)
    target = flat_ids * CAP + slot_pos
    block_idx = jnp.arange(blocks, dtype=jnp.int32)[:, None]
    packed = jnp.zeros((blocks, EXPERTS * CAP, D), jnp.bfloat16).at[block_idx, target].set(scaled)
    packed = packed.reshape(N_REPLICA, ndev, EXPERTS, CAP, D)
    gate_w = w_gate.reshape(N_GROUP // 2, 2, N_EXPERT, D, FFH)
    up_w = w_up.reshape(N_GROUP // 2, 2, N_EXPERT, D, FFH)
    down_w = w_down.reshape(N_GROUP // 2, 2, N_EXPERT, FFH, D)
    gate_saved = saved_gate.reshape(N_GROUP // 2, 2, N_EXPERT, N_REPLICA, SLOTS, FFH)
    up_saved = saved_up.reshape(N_GROUP // 2, 2, N_EXPERT, N_REPLICA, SLOTS, FFH)

    def per_expert(expert):
        pair_idx = expert // N_EXPERT
        column = expert % N_EXPERT
        rows_dy = lax.dynamic_index_in_dim(packed, expert, axis=2, keepdims=False)
        rows_dy = rows_dy.reshape(N_REPLICA, SLOTS, D).astype(jnp.float32)
        partials = []
        grads = []
        for half_idx in range(2):
            pre_gate = gate_saved[pair_idx, half_idx, column].astype(jnp.float32)
            pre_up = up_saved[pair_idx, half_idx, column].astype(jnp.float32)
            sigmoid_gate = jax.nn.sigmoid(pre_gate)
            silu_gate = pre_gate * sigmoid_gate
            activation = (silu_gate * pre_up).astype(jnp.bfloat16).astype(jnp.float32)
            down_f = down_w[pair_idx, half_idx, column].astype(jnp.float32)
            d_act = jnp.einsum('rsd,fd->rsf', rows_dy, down_f)
            d_gate = (d_act * pre_up * sigmoid_gate * (1.0 + pre_gate * (1.0 - sigmoid_gate))).astype(jnp.bfloat16)
            d_up = (d_act * silu_gate).astype(jnp.bfloat16)
            partial_value = jnp.einsum('rsf,df->rsd', d_gate.astype(jnp.float32), gate_w[pair_idx, half_idx, column].astype(jnp.float32))
            partial_value = partial_value + jnp.einsum('rsf,df->rsd', d_up.astype(jnp.float32), up_w[pair_idx, half_idx, column].astype(jnp.float32))
            partials.append(partial_value.astype(jnp.bfloat16).astype(jnp.float32))
            grad_terms = jnp.einsum('rsf,rsd->rfd', activation, rows_dy)
            grads.append(jnp.sum(grad_terms, axis=0))
        combined = (partials[0] + partials[1]).astype(jnp.bfloat16)
        return combined, jnp.stack(grads)

    combined_all, grads_all = lax.map(per_expert, jnp.arange(EXPERTS, dtype=jnp.int32))
    replica_of = (jnp.arange(blocks, dtype=jnp.int32) // ndev)[:, None]
    source_of = (jnp.arange(blocks, dtype=jnp.int32) % ndev)[:, None]
    gathered = combined_all[flat_ids, replica_of, source_of * CAP + slot_pos]
    gathered = gathered.reshape(N_REPLICA, ndev * TOK_DEV, KREP, D).astype(jnp.float32)
    grad_input = jnp.sum(gathered, axis=(0, 2)).astype(jnp.bfloat16)
    grad_down = grads_all.reshape(N_GROUP // 2, N_EXPERT, 2, FFH, D).transpose(0, 2, 1, 3, 4).reshape(UNITS, FFH, D)
    return grad_input, grad_down
```

```python
import functools

import jax
import jax.numpy as jnp
from jax import lax
from jax.experimental import pallas as pl
from jax.experimental.pallas import tpu as pltpu
from jax.sharding import PartitionSpec as P

MESH = pl.DeviceIdType.MESH
NT = (((1,), (1,)), ((), ()))


def from_partner(value, axis, bit):
    mask = 2**bit
    pairs = [(source, source ^ mask) for source in range(lax.axis_size(axis))]
    return lax.ppermute(value, axis, pairs)


def routed_plan(cotangent, expert_ids, gate_probs, saved_gate, saved_up, w_gate, w_up, w_down):
    n_group = lax.axis_size("group")
    n_expert = lax.axis_size("expert")
    tok_rows, model_width = cotangent.shape
    pick_count = expert_ids.shape[2]
    experts = n_group * n_expert // 2
    half_width = model_width // 2
    capacity = saved_gate.shape[1] // (n_group * n_expert)
    assigned = tok_rows * pick_count
    flat_ids = expert_ids.reshape(assigned)
    positions = jnp.arange(assigned, dtype=jnp.int32)
    same_expert = (flat_ids[:, None] == flat_ids[None, :]) & (
        positions[None, :] < positions[:, None]
    )
    slot_pos = jnp.sum(same_expert.astype(jnp.int32), axis=1)
    target = flat_ids * capacity + slot_pos
    places = jnp.arange(experts * capacity, dtype=jnp.int32)
    dispatch_map = (places[:, None] == target[None, :]).astype(jnp.bfloat16)
    scaled = (gate_probs[0][:, :, None] * cotangent[:, None, :].astype(jnp.float32)).astype(
        jnp.bfloat16
    )
    scaled = scaled.reshape(assigned, model_width)
    packed = jnp.dot(dispatch_map, scaled, preferred_element_type=jnp.float32).astype(jnp.bfloat16)
    packed = packed.reshape(n_group // 2, n_expert, capacity, 2, half_width)
    packed = packed.transpose(0, 3, 1, 2, 4).reshape(n_group, n_expert, capacity, half_width)
    arrived = lax.all_to_all(
        lax.all_to_all(packed, "expert", split_axis=1, concat_axis=1, tiled=True),
        "group",
        split_axis=0,
        concat_axis=0,
        tiled=True,
    )
    partner = from_partner(arrived, "group", 0)
    low_half = lax.axis_index("group") % 2 == 0
    front_half = jnp.where(low_half, arrived, partner)
    back_half = jnp.where(low_half, partner, arrived)
    dy_slots = jnp.concatenate([front_half, back_half], axis=3).reshape(-1, model_width)
    pre_gate = saved_gate[0].astype(jnp.float32)
    pre_up = saved_up[0].astype(jnp.float32)
    sigmoid_gate = jax.nn.sigmoid(pre_gate)
    silu_gate = pre_gate * sigmoid_gate
    activation = (silu_gate * pre_up).astype(jnp.bfloat16)
    d_act = lax.dot_general(
        dy_slots, w_down[0], (((1,), (1,)), ((), ())), preferred_element_type=jnp.float32
    )
    d_gate = (d_act * pre_up * sigmoid_gate * (1.0 + pre_gate * (1.0 - sigmoid_gate))).astype(
        jnp.bfloat16
    )
    d_up = (d_act * silu_gate).astype(jnp.bfloat16)
    partial_value = lax.dot_general(
        d_gate, w_gate[0], (((1,), (1,)), ((), ())), preferred_element_type=jnp.float32
    )
    partial_value = partial_value + lax.dot_general(
        d_up, w_up[0], (((1,), (1,)), ((), ())), preferred_element_type=jnp.float32
    )
    partial_value = partial_value.astype(jnp.bfloat16)
    own_half = jnp.where(low_half, partial_value[:, :half_width], partial_value[:, half_width:])
    peer_half = jnp.where(low_half, partial_value[:, half_width:], partial_value[:, :half_width])
    received = from_partner(peer_half, "group", 0)
    combined = (own_half.astype(jnp.float32) + received.astype(jnp.float32)).astype(jnp.bfloat16)
    combined = combined.reshape(n_group, n_expert, capacity, half_width)
    grad_terms = lax.dot_general(
        activation, dy_slots, (((0,), (0,)), ((), ())), preferred_element_type=jnp.float32
    )
    returned = lax.all_to_all(
        lax.all_to_all(combined, "group", split_axis=0, concat_axis=0, tiled=True),
        "expert",
        split_axis=1,
        concat_axis=1,
        tiled=True,
    )
    home_rows = returned.reshape(n_group // 2, 2, n_expert, capacity, half_width)
    home_rows = home_rows.transpose(0, 2, 3, 1, 4).reshape(experts * capacity, model_width)
    per_assign = lax.dot_general(
        dispatch_map, home_rows, (((0,), (0,)), ((), ())), preferred_element_type=jnp.float32
    )
    home_sum = jnp.sum(per_assign.reshape(tok_rows, pick_count, model_width), axis=1)
    grad_down, grad_input = (
        lax.psum_scatter(grad_terms, "replica", scatter_dimension=1, tiled=True),
        lax.psum_scatter(home_sum, "replica", scatter_dimension=1, tiled=True),
    )
    return (grad_input.astype(jnp.bfloat16), grad_down[None])


def dense_kernel(
    n_group,
    n_expert,
    cot_ref,
    ids_ref,
    prob_ref,
    sg_ref,
    su_ref,
    wg_ref,
    wu_ref,
    wd_ref,
    out_ref,
    gd_ref,
    cot_all,
    meta_all,
    act_t,
    f_gate,
    f_up,
    own_buf,
    sib_send,
    sib_recv,
    p_buf,
    ra,
    rb,
    a2,
    b2,
    ra2,
    rb2,
    z_send,
    z_recv,
    gt_send,
    gt_recv,
    ssem,
    rsem,
    gsem,
    lsem,
):
    tok, width = cot_ref.shape
    half = width // 2
    quarter = half // 2
    rows_g = n_expert * tok
    picks = ids_ref.shape[1]
    experts = meta_all.shape[1]
    f32, bf16 = jnp.float32, jnp.bfloat16
    g = lax.axis_index("group")
    ex = lax.axis_index("expert")
    r = lax.axis_index("replica")
    x, y = ex % 2, ex // 2
    nx, ny = 1 - x, 1 - y
    ex_x, ex_y, ex_d = y * 2 + nx, ny * 2 + x, ny * 2 + nx
    x_dev, y_dev, d_dev = (g, ex_x, r), (g, ex_y, r), (g, ex_d, r)
    sib_dev = (g, ex, 1 - r)

    def group_at(i):
        low = (g % 2 + i % 2) % 2
        high = (g // 2 + i // 2) % 2
        return low + 2 * high

    my_col = pl.multiple_of(r * half, half)
    sib_col = pl.multiple_of((1 - r) * half, half)
    col_a = my_col
    col_b = pl.multiple_of(r * half + quarter, quarter)

    def row_of(q, e):
        return pl.multiple_of((q * n_expert + e) * tok, tok)

    def rcopy(kind, i, src, dst, dev):
        return pltpu.make_async_remote_copy(
            src_ref=src,
            dst_ref=dst,
            send_sem=ssem.at[kind, i],
            recv_sem=rsem.at[kind, i],
            device_id=dev,
            device_id_type=MESH,
        )

    def block(q, e, col, size):
        return cot_all.at[pl.ds(row_of(q, e), tok), pl.ds(col, size)]

    def z_dev(i):
        return (group_at(i), ex, r)

    def ag_z(i, recv):
        land = block(group_at(i), ex, my_col, half) if recv else block(g, ex, my_col, half)
        src = land if recv else cot_ref.at[:, pl.ds(my_col, half)]
        return rcopy(0, i, src, land, z_dev(i))

    def ag_mz(i, recv):
        ref = meta_all.at[(group_at(i) if recv else g) * n_expert + ex]
        return rcopy(1, i, ref, ref, z_dev(i))

    def ag_xy(kind, i, e, col, dev):
        ref = block(group_at(i), e, col, quarter)
        return rcopy(kind, i, ref, ref, dev)

    def ag_meta(kind, i, e, dev):
        ref = meta_all.at[group_at(i) * n_expert + e]
        return rcopy(kind, i, ref, ref, dev)

    def ag_sib(i, recv):
        rows = pl.ds(row_of(group_at(i), 0), rows_g)
        ref = cot_all.at[rows, pl.ds(sib_col if recv else my_col, half)]
        return rcopy(11, i, ref, ref, sib_dev)

    def rs_sib(i):
        return rcopy(12, i, sib_send.at[i], sib_recv.at[i], sib_dev)

    def rs_a1(i):
        return rcopy(13, i, p_buf.at[i, ny, :, :, pl.ds(0, quarter)], ra.at[i], y_dev)

    def rs_b1(i):
        return rcopy(14, i, p_buf.at[i, :, nx, :, pl.ds(quarter, quarter)], rb.at[i], x_dev)

    def rs_a2(i):
        return rcopy(15, i, a2.at[i, nx], ra2.at[i], x_dev)

    def rs_b2(i):
        return rcopy(16, i, b2.at[i, ny], rb2.at[i], y_dev)

    def rs_z(i):
        return rcopy(17, i, z_send.at[i], z_recv.at[i], z_dev(i))

    grad_copy = pltpu.make_async_remote_copy(
        src_ref=gt_send,
        dst_ref=gt_recv,
        send_sem=gsem.at[0],
        recv_sem=gsem.at[1],
        device_id=sib_dev,
        device_id_type=MESH,
    )

    barrier = pltpu.get_barrier_semaphore()
    peers = [z_dev(i) for i in range(1, n_group)] + [x_dev, y_dev, d_dev, sib_dev]
    for dev in peers:
        pl.semaphore_signal(barrier, inc=1, device_id=dev, device_id_type=MESH)

    place = pltpu.make_async_copy(
        cot_ref.at[:, pl.ds(my_col, half)], block(g, ex, my_col, half), lsem
    )
    place.start()
    lane = lax.broadcasted_iota(jnp.int32, (tok, 128), 1)
    named = jnp.zeros((tok, 128), f32)
    weight = jnp.zeros((tok, 128), f32)
    for k in range(picks):
        same = ids_ref[:, k : k + 1] == lane
        named = named + jnp.where(same, 1.0, 0.0)
        weight = weight + jnp.where(same, prob_ref[:, k : k + 1], 0.0)
    before = lax.broadcasted_iota(jnp.int32, (tok, tok), 0) > lax.broadcasted_iota(
        jnp.int32, (tok, tok), 1
    )
    slot = jnp.dot(
        jnp.where(before, 1.0, 0.0).astype(bf16), named.astype(bf16), preferred_element_type=f32
    )
    slot = jnp.where(named > 0.5, slot, -1.0)
    meta_all[g * n_expert + ex] = jnp.concatenate([slot, weight], axis=0).T[:experts]
    place.wait()
    pl.semaphore_wait(barrier, len(peers))

    for i in range(1, n_group):
        ag_mz(i, False).start()
    for i in range(1, n_group):
        ag_z(i, False).start()

    expert = (g // 2) * n_expert + ex
    eye = lax.broadcasted_iota(jnp.int32, (2 * tok, 2 * tok), 0) == lax.broadcasted_iota(
        jnp.int32, (2 * tok, 2 * tok), 1
    )
    place_lane = lax.broadcasted_iota(jnp.int32, (tok, rows_g), 1).astype(f32)

    def ag_first(i):
        @pl.when(i > 0)
        def _():
            ag_mz(i, True).wait_recv()
            ag_z(i, True).wait_recv()

        ag_meta(8, i, ex, x_dev).start()
        ag_meta(9, i, ex, y_dev).start()
        ag_meta(10, i, ex, d_dev).start()
        ag_xy(2, i, ex, col_a, x_dev).start()
        ag_xy(3, i, ex, col_b, y_dev).start()
        ag_xy(4, i, ex, col_b, x_dev).start()
        ag_xy(5, i, ex, col_a, y_dev).start()

    def ag_second(i):
        ag_xy(2, i, ex_x, col_a, x_dev).wait_recv()
        ag_xy(6, i, ex_x, col_a, y_dev).start()
        ag_xy(3, i, ex_y, col_b, y_dev).wait_recv()
        ag_xy(7, i, ex_y, col_b, x_dev).start()

    def ag_third(i):
        q = group_at(i)
        ag_meta(8, i, ex_x, x_dev).wait_recv()
        ag_meta(9, i, ex_y, y_dev).wait_recv()
        ag_meta(10, i, ex_d, d_dev).wait_recv()
        picked, weights = [], []
        for b in range(n_expert):
            row = meta_all[q * n_expert + b, pl.ds(expert, 1), :]
            col = jnp.sum(jnp.where(eye, row, 0.0), axis=1, keepdims=True)
            slot_col = col[:tok]
            target = jnp.where(slot_col < -0.5, -1.0, slot_col + float(b * tok))
            picked.append(jnp.where(place_lane == target, 1.0, 0.0))
            weights.append(col[tok:])
        select = jnp.concatenate(picked, axis=0).astype(bf16)
        weights = jnp.concatenate(weights, axis=0)
        rows = pl.ds(pl.multiple_of(q * rows_g, rows_g), rows_g)
        gate = jnp.dot(select, sg_ref[0, rows, :], preferred_element_type=f32)
        up = jnp.dot(select, su_ref[0, rows, :], preferred_element_type=f32)
        sig = jax.nn.sigmoid(gate)
        silu = gate * sig
        act_t[:, rows] = (silu * up * weights).T.astype(bf16)
        f_gate[i] = weights * up * sig * (1.0 + gate * (1.0 - sig))
        f_up[i] = weights * silu
        ag_xy(4, i, ex_x, col_b, x_dev).wait_recv()
        ag_xy(5, i, ex_y, col_a, y_dev).wait_recv()
        ag_xy(6, i, ex_d, col_a, y_dev).wait_recv()
        ag_xy(7, i, ex_d, col_b, x_dev).wait_recv()
        ag_sib(i, False).start()

    def compute(i):
        q = group_at(i)
        ag_sib(i, True).wait_recv()
        rows = pl.ds(pl.multiple_of(q * rows_g, rows_g), rows_g)
        d_act = lax.dot_general(
            cot_all[rows, :], wd_ref[0], NT, preferred_element_type=f32
        )
        d_gate = (d_act * f_gate[i]).astype(bf16)
        d_up = (d_act * f_up[i]).astype(bf16)

        def partial_of(col):
            wide = pl.ds(col, half)
            value = lax.dot_general(d_gate, wg_ref[0, wide, :], NT, preferred_element_type=f32)
            return value + lax.dot_general(
                d_up, wu_ref[0, wide, :], NT, preferred_element_type=f32
            )

        sib_send[i] = partial_of(sib_col).astype(bf16)
        rs_sib(i).start()
        own_buf[i] = partial_of(my_col).astype(bf16)

    def rs_first(i):
        rs_sib(i).wait_recv()
        total = own_buf[i].astype(f32) + sib_recv[i].astype(f32)
        p_buf[i] = total.astype(bf16).reshape(2, 2, tok, half)
        rs_a1(i).start()
        rs_b1(i).start()

    def rs_second(i):
        rs_a1(i).wait_recv()
        left = p_buf[i, y, :, :, pl.ds(0, quarter)].astype(f32) + ra[i].astype(f32)
        a2[i] = left.astype(bf16)
        rs_a2(i).start()
        rs_b1(i).wait_recv()
        right = p_buf[i, :, x, :, pl.ds(quarter, quarter)].astype(f32) + rb[i].astype(f32)
        b2[i] = right.astype(bf16)
        rs_b2(i).start()

    def rs_third(i):
        rs_a2(i).wait_recv()
        rs_b2(i).wait_recv()
        left = a2[i, x].astype(f32) + ra2[i].astype(f32)
        right = b2[i, y].astype(f32) + rb2[i].astype(f32)
        z_send[i] = jnp.concatenate([left, right], axis=1).astype(bf16)

        @pl.when(i > 0)
        def _():
            rs_z(i).start()

    def grad_chunk(j):
        base = jnp.where(j < 2, 1 - r, r) * half + (j % 2) * quarter
        cols = pl.ds(pl.multiple_of(base, quarter), quarter)
        value = jnp.dot(act_t[...], cot_all[:, cols], preferred_element_type=f32)
        land = pl.ds(pl.multiple_of((j % 2) * quarter, quarter), quarter)

        @pl.when(j < 2)
        def _():
            gt_send[:, land] = value.astype(bf16)

        @pl.when(j >= 2)
        def _():
            gd_ref[0, :, land] = value

        @pl.when(j == 1)
        def _():
            grad_copy.start()

    stages = (ag_first, ag_second, ag_third, compute, rs_first, rs_second, rs_third)
    order = (0, 1, 4, 5, 6, 2, 3)
    last = n_group + len(stages) - 1

    def step(s, carry):
        for lag in order:

            @pl.when((s >= lag) & (s < lag + n_group))
            def _(lag=lag):
                stages[lag](s - lag)

        @pl.when(s >= last - 4)
        def _():
            grad_chunk(s - (last - 4))

        return carry

    lax.fori_loop(0, last, step, 0)

    grad_copy.wait_recv()
    gd_ref[0] = gd_ref[0] + gt_recv[...].astype(f32)
    total = z_send[0].astype(f32)
    for i in range(1, n_group):
        rs_z(i).wait_recv()
        total = total + z_recv[i].astype(f32)
    out_ref[...] = total.astype(bf16)

    grad_copy.wait_send()

    def drain(i, carry):
        @pl.when(i > 0)
        def _():
            ag_z(i, False).wait_send()
            ag_mz(i, False).wait_send()
            rs_z(i).wait_send()

        ag_meta(8, i, ex, x_dev).wait_send()
        ag_meta(9, i, ex, y_dev).wait_send()
        ag_meta(10, i, ex, d_dev).wait_send()
        ag_xy(2, i, ex, col_a, x_dev).wait_send()
        ag_xy(3, i, ex, col_b, y_dev).wait_send()
        ag_xy(4, i, ex, col_b, x_dev).wait_send()
        ag_xy(5, i, ex, col_a, y_dev).wait_send()
        ag_xy(6, i, ex_x, col_a, y_dev).wait_send()
        ag_xy(7, i, ex_y, col_b, x_dev).wait_send()
        ag_sib(i, False).wait_send()
        rs_sib(i).wait_send()
        rs_a1(i).wait_send()
        rs_b1(i).wait_send()
        rs_a2(i).wait_send()
        rs_b2(i).wait_send()
        return carry

    lax.fori_loop(0, n_group, drain, 0)


def dense_plan(cotangent, expert_ids, gate_probs, saved_gate, saved_up, w_gate, w_up, w_down):
    n_group = lax.axis_size("group")
    n_expert = lax.axis_size("expert")
    tok, width = cotangent.shape
    half, quarter = width // 2, width // 4
    hidden = w_down.shape[1]
    experts = n_group * n_expert // 2
    blocks = n_group * n_expert
    rows_g = n_expert * tok
    bf16, f32 = jnp.bfloat16, jnp.float32
    vmem = pl.BlockSpec(memory_space=pltpu.VMEM)
    kinds = 18
    return pl.pallas_call(
        functools.partial(dense_kernel, n_group, n_expert),
        out_shape=(
            jax.ShapeDtypeStruct((tok, half), bf16),
            jax.ShapeDtypeStruct((1, hidden, half), f32),
        ),
        in_specs=[vmem] * 8,
        out_specs=(vmem, vmem),
        scratch_shapes=[
            pltpu.VMEM((blocks * tok, width), bf16),
            pltpu.VMEM((blocks, experts, 2 * tok), f32),
            pltpu.VMEM((hidden, blocks * tok), bf16),
            pltpu.VMEM((n_group, rows_g, hidden), f32),
            pltpu.VMEM((n_group, rows_g, hidden), f32),
            pltpu.VMEM((n_group, rows_g, half), bf16),
            pltpu.VMEM((n_group, rows_g, half), bf16),
            pltpu.VMEM((n_group, rows_g, half), bf16),
            pltpu.VMEM((n_group, 2, 2, tok, half), bf16),
            pltpu.VMEM((n_group, 2, tok, quarter), bf16),
            pltpu.VMEM((n_group, 2, tok, quarter), bf16),
            pltpu.VMEM((n_group, 2, tok, quarter), bf16),
            pltpu.VMEM((n_group, 2, tok, quarter), bf16),
            pltpu.VMEM((n_group, tok, quarter), bf16),
            pltpu.VMEM((n_group, tok, quarter), bf16),
            pltpu.VMEM((n_group, tok, half), bf16),
            pltpu.VMEM((n_group, tok, half), bf16),
            pltpu.VMEM((hidden, half), bf16),
            pltpu.VMEM((hidden, half), bf16),
            pltpu.SemaphoreType.DMA((kinds, n_group)),
            pltpu.SemaphoreType.DMA((kinds, n_group)),
            pltpu.SemaphoreType.DMA((2,)),
            pltpu.SemaphoreType.DMA,
        ],
        compiler_params=pltpu.CompilerParams(
            collective_id=0, has_side_effects=True, vmem_limit_bytes=60 * 1024 * 1024
        ),
    )(
        cotangent,
        expert_ids[0],
        gate_probs[0],
        saved_gate,
        saved_up,
        w_gate,
        w_up,
        w_down,
    )


def on_device(cotangent, expert_ids, gate_probs, saved_gate, saved_up, w_gate, w_up, w_down):
    n_group = lax.axis_size("group")
    n_expert = lax.axis_size("expert")
    n_replica = lax.axis_size("replica")
    tok_rows = cotangent.shape[0]
    capacity = saved_gate.shape[1] // (n_group * n_expert)
    small = n_group == 4 and n_expert == 4 and n_replica == 2
    plan = routed_plan
    if small and capacity == tok_rows and 2 * tok_rows == 128:
        plan = dense_plan
    return plan(cotangent, expert_ids, gate_probs, saved_gate, saved_up, w_gate, w_up, w_down)


def solution(mesh):
    return jax.shard_map(
        on_device,
        mesh=mesh,
        in_specs=(
            P(("group", "expert"), None),
            P("replica", ("group", "expert"), None),
            P("replica", ("group", "expert"), None),
            P(("group", "expert"), "replica", None),
            P(("group", "expert"), "replica", None),
            P(("group", "expert"), None, None),
            P(("group", "expert"), None, None),
            P(("group", "expert"), None, None),
        ),
        out_specs=(P(("group", "expert"), "replica"), P(("group", "expert"), None, "replica")),
        check_vma=False,
    )
```

```python
import functools

import jax
import jax.numpy as jnp
from jax import lax
from jax.experimental import pallas as pl
from jax.experimental.pallas import tpu as pltpu
from jax.sharding import PartitionSpec as P

MESH = pl.DeviceIdType.MESH
NT = (((1,), (1,)), ((), ()))


def from_partner(value, axis, bit):
    mask = 2**bit
    pairs = [(source, source ^ mask) for source in range(lax.axis_size(axis))]
    return lax.ppermute(value, axis, pairs)


def routed_plan(cotangent, expert_ids, gate_probs, saved_gate, saved_up, w_gate, w_up, w_down):
    n_group = lax.axis_size("group")
    n_expert = lax.axis_size("expert")
    tok_rows, model_width = cotangent.shape
    pick_count = expert_ids.shape[2]
    experts = n_group * n_expert // 2
    half_width = model_width // 2
    capacity = saved_gate.shape[1] // (n_group * n_expert)
    assigned = tok_rows * pick_count
    flat_ids = expert_ids.reshape(assigned)
    positions = jnp.arange(assigned, dtype=jnp.int32)
    same_expert = (flat_ids[:, None] == flat_ids[None, :]) & (
        positions[None, :] < positions[:, None]
    )
    slot_pos = jnp.sum(same_expert.astype(jnp.int32), axis=1)
    target = flat_ids * capacity + slot_pos
    places = jnp.arange(experts * capacity, dtype=jnp.int32)
    dispatch_map = (places[:, None] == target[None, :]).astype(jnp.bfloat16)
    scaled = (gate_probs[0][:, :, None] * cotangent[:, None, :].astype(jnp.float32)).astype(
        jnp.bfloat16
    )
    scaled = scaled.reshape(assigned, model_width)
    packed = jnp.dot(dispatch_map, scaled, preferred_element_type=jnp.float32).astype(jnp.bfloat16)
    packed = packed.reshape(n_group // 2, n_expert, capacity, 2, half_width)
    packed = packed.transpose(0, 3, 1, 2, 4).reshape(n_group, n_expert, capacity, half_width)
    arrived = lax.all_to_all(
        lax.all_to_all(packed, "expert", split_axis=1, concat_axis=1, tiled=True),
        "group",
        split_axis=0,
        concat_axis=0,
        tiled=True,
    )
    partner = from_partner(arrived, "group", 0)
    low_half = lax.axis_index("group") % 2 == 0
    front_half = jnp.where(low_half, arrived, partner)
    back_half = jnp.where(low_half, partner, arrived)
    dy_slots = jnp.concatenate([front_half, back_half], axis=3).reshape(-1, model_width)
    pre_gate = saved_gate[0].astype(jnp.float32)
    pre_up = saved_up[0].astype(jnp.float32)
    sigmoid_gate = jax.nn.sigmoid(pre_gate)
    silu_gate = pre_gate * sigmoid_gate
    activation = (silu_gate * pre_up).astype(jnp.bfloat16)
    d_act = lax.dot_general(
        dy_slots, w_down[0], (((1,), (1,)), ((), ())), preferred_element_type=jnp.float32
    )
    d_gate = (d_act * pre_up * sigmoid_gate * (1.0 + pre_gate * (1.0 - sigmoid_gate))).astype(
        jnp.bfloat16
    )
    d_up = (d_act * silu_gate).astype(jnp.bfloat16)
    partial_value = lax.dot_general(
        d_gate, w_gate[0], (((1,), (1,)), ((), ())), preferred_element_type=jnp.float32
    )
    partial_value = partial_value + lax.dot_general(
        d_up, w_up[0], (((1,), (1,)), ((), ())), preferred_element_type=jnp.float32
    )
    partial_value = partial_value.astype(jnp.bfloat16)
    own_half = jnp.where(low_half, partial_value[:, :half_width], partial_value[:, half_width:])
    peer_half = jnp.where(low_half, partial_value[:, half_width:], partial_value[:, :half_width])
    received = from_partner(peer_half, "group", 0)
    combined = (own_half.astype(jnp.float32) + received.astype(jnp.float32)).astype(jnp.bfloat16)
    combined = combined.reshape(n_group, n_expert, capacity, half_width)
    grad_terms = lax.dot_general(
        activation, dy_slots, (((0,), (0,)), ((), ())), preferred_element_type=jnp.float32
    )
    returned = lax.all_to_all(
        lax.all_to_all(combined, "group", split_axis=0, concat_axis=0, tiled=True),
        "expert",
        split_axis=1,
        concat_axis=1,
        tiled=True,
    )
    home_rows = returned.reshape(n_group // 2, 2, n_expert, capacity, half_width)
    home_rows = home_rows.transpose(0, 2, 3, 1, 4).reshape(experts * capacity, model_width)
    per_assign = lax.dot_general(
        dispatch_map, home_rows, (((0,), (0,)), ((), ())), preferred_element_type=jnp.float32
    )
    home_sum = jnp.sum(per_assign.reshape(tok_rows, pick_count, model_width), axis=1)
    grad_down, grad_input = (
        lax.psum_scatter(grad_terms, "replica", scatter_dimension=1, tiled=True),
        lax.psum_scatter(home_sum, "replica", scatter_dimension=1, tiled=True),
    )
    return (grad_input.astype(jnp.bfloat16), grad_down[None])


def dense_kernel(
    n_group,
    n_expert,
    cot_ref,
    ids_ref,
    prob_ref,
    sg_hbm,
    su_hbm,
    wg_hbm,
    wu_hbm,
    wd_hbm,
    out_ref,
    gd_ref,
    gt_recv,
    sg_ref,
    su_ref,
    wg_ref,
    wu_ref,
    wd_ref,
    cot_all,
    meta_all,
    act_t,
    f_gate,
    f_up,
    own_buf,
    sib_send,
    sib_recv,
    p_buf,
    ra,
    rb,
    a2,
    b2,
    ra2,
    rb2,
    z_send,
    z_recv,
    gt_send,
    ssem,
    rsem,
    gsem,
    lsem,
):
    tok, width = cot_ref.shape
    half = width // 2
    quarter = half // 2
    rows_g = n_expert * tok
    picks = ids_ref.shape[0]
    experts = meta_all.shape[1]
    f32, bf16 = jnp.float32, jnp.bfloat16
    g = lax.axis_index("group")
    ex = lax.axis_index("expert")
    r = lax.axis_index("replica")
    x, y = ex % 2, ex // 2
    nx, ny = 1 - x, 1 - y
    ex_x, ex_y, ex_d = y * 2 + nx, ny * 2 + x, ny * 2 + nx
    x_dev, y_dev, d_dev = (g, ex_x, r), (g, ex_y, r), (g, ex_d, r)
    sib_dev = (g, ex, 1 - r)

    def group_at(i):
        low = (g % 2 + i % 2) % 2
        high = (g // 2 + i // 2) % 2
        return low + 2 * high

    my_col = pl.multiple_of(r * half, half)
    sib_col = pl.multiple_of((1 - r) * half, half)
    col_a = my_col
    col_b = pl.multiple_of(r * half + quarter, quarter)

    def row_of(q, e):
        return pl.multiple_of((q * n_expert + e) * tok, tok)

    def rcopy(kind, i, src, dst, dev):
        return pltpu.make_async_remote_copy(
            src_ref=src,
            dst_ref=dst,
            send_sem=ssem.at[kind, i],
            recv_sem=rsem.at[kind, i],
            device_id=dev,
            device_id_type=MESH,
        )

    def block(q, e, col, size):
        return cot_all.at[pl.ds(row_of(q, e), tok), pl.ds(col, size)]

    def z_dev(i):
        return (group_at(i), ex, r)

    def ag_z(i, recv):
        land = block(group_at(i), ex, my_col, half) if recv else block(g, ex, my_col, half)
        return rcopy(0, i, land, land, z_dev(i))

    def ag_mz(i, recv):
        ref = meta_all.at[(group_at(i) if recv else g) * n_expert + ex]
        return rcopy(1, i, ref, ref, z_dev(i))

    def ag_xy(kind, i, e, col, dev):
        ref = block(group_at(i), e, col, quarter)
        return rcopy(kind, i, ref, ref, dev)

    def ag_meta(kind, i, e, dev):
        ref = meta_all.at[group_at(i) * n_expert + e]
        return rcopy(kind, i, ref, ref, dev)

    def ag_sib(i, recv):
        rows = pl.ds(row_of(group_at(i), 0), rows_g)
        ref = cot_all.at[rows, pl.ds(sib_col if recv else my_col, half)]
        return rcopy(11, i, ref, ref, sib_dev)

    def rs_sib(i):
        return rcopy(12, i, sib_send.at[i], sib_recv.at[i], sib_dev)

    def rs_a1(i):
        return rcopy(13, i, p_buf.at[i, ny, :, :, pl.ds(0, quarter)], ra.at[i], y_dev)

    def rs_b1(i):
        return rcopy(14, i, p_buf.at[i, :, nx, :, pl.ds(quarter, quarter)], rb.at[i], x_dev)

    def rs_a2(i):
        return rcopy(15, i, a2.at[i, nx], ra2.at[i], x_dev)

    def rs_b2(i):
        return rcopy(16, i, b2.at[i, ny], rb2.at[i], y_dev)

    def rs_z(i):
        return rcopy(17, i, z_send.at[i], z_recv.at[i], z_dev(i))

    grad_copy = pltpu.make_async_remote_copy(
        src_ref=gt_send,
        dst_ref=gt_recv,
        send_sem=gsem.at[0],
        recv_sem=gsem.at[1],
        device_id=sib_dev,
        device_id_type=MESH,
    )

    barrier = pltpu.get_barrier_semaphore()
    peers = [z_dev(i) for i in range(1, n_group)] + [x_dev, y_dev, d_dev, sib_dev]
    for dev in peers:
        pl.semaphore_signal(barrier, inc=1, device_id=dev, device_id_type=MESH)

    place = pltpu.make_async_copy(
        cot_ref.at[:, pl.ds(my_col, half)], block(g, ex, my_col, half), lsem.at[0]
    )
    place.start()
    loads = [
        pltpu.make_async_copy(src, dst, lsem.at[1 + k])
        for k, (src, dst) in enumerate(
            [
                (sg_hbm, sg_ref),
                (su_hbm, su_ref),
                (wd_hbm, wd_ref),
                (wg_hbm, wg_ref),
                (wu_hbm, wu_ref),
            ]
        )
    ]
    for load in loads:
        load.start()
    named_by = lax.broadcasted_iota(jnp.int32, (experts, tok), 0)
    named = jnp.zeros((experts, tok), f32)
    weight = jnp.zeros((experts, tok), f32)
    for k in range(picks):
        same = ids_ref[k : k + 1, :] == named_by
        named = named + jnp.where(same, 1.0, 0.0)
        weight = weight + jnp.where(same, prob_ref[k : k + 1, :], 0.0)
    before = lax.broadcasted_iota(jnp.int32, (tok, tok), 0) < lax.broadcasted_iota(
        jnp.int32, (tok, tok), 1
    )
    slot = jnp.dot(
        named.astype(bf16), jnp.where(before, 1.0, 0.0).astype(bf16), preferred_element_type=f32
    )
    slot = jnp.where(named > 0.5, slot, -1.0)
    meta_all[g * n_expert + ex] = jnp.concatenate([slot, weight], axis=1)
    place.wait()
    pl.semaphore_wait(barrier, len(peers))

    for i in range(1, n_group):
        ag_mz(i, False).start()
    for i in range(1, n_group):
        ag_z(i, False).start()

    expert = (g // 2) * n_expert + ex
    eye = lax.broadcasted_iota(jnp.int32, (2 * tok, 2 * tok), 0) == lax.broadcasted_iota(
        jnp.int32, (2 * tok, 2 * tok), 1
    )
    place_lane = lax.broadcasted_iota(jnp.int32, (tok, rows_g), 1).astype(f32)

    def ag_first(i):
        @pl.when(i > 0)
        def _():
            ag_mz(i, True).wait_recv()
            ag_z(i, True).wait_recv()

        ag_meta(8, i, ex, x_dev).start()
        ag_meta(9, i, ex, y_dev).start()
        ag_meta(10, i, ex, d_dev).start()
        ag_xy(2, i, ex, col_a, x_dev).start()
        ag_xy(3, i, ex, col_b, y_dev).start()
        ag_xy(4, i, ex, col_b, x_dev).start()
        ag_xy(5, i, ex, col_a, y_dev).start()

    def ag_second(i):
        ag_xy(2, i, ex_x, col_a, x_dev).wait_recv()
        ag_xy(6, i, ex_x, col_a, y_dev).start()
        ag_xy(3, i, ex_y, col_b, y_dev).wait_recv()
        ag_xy(7, i, ex_y, col_b, x_dev).start()

    def ag_third(i):
        q = group_at(i)
        ag_meta(8, i, ex_x, x_dev).wait_recv()
        ag_meta(9, i, ex_y, y_dev).wait_recv()
        ag_meta(10, i, ex_d, d_dev).wait_recv()
        picked, weights = [], []
        for b in range(n_expert):
            row = meta_all[q * n_expert + b, pl.ds(expert, 1), :]
            col = jnp.sum(jnp.where(eye, row, 0.0), axis=1, keepdims=True)
            slot_col = col[:tok]
            target = jnp.where(slot_col < -0.5, -1.0, slot_col + float(b * tok))
            picked.append(jnp.where(place_lane == target, 1.0, 0.0))
            weights.append(col[tok:])
        select = jnp.concatenate(picked, axis=0).astype(bf16)
        weights = jnp.concatenate(weights, axis=0)
        rows = pl.ds(pl.multiple_of(q * rows_g, rows_g), rows_g)

        @pl.when(i == 0)
        def _():
            for load in loads[:2]:
                load.wait()

        gate = jnp.dot(select, sg_ref[0, rows, :], preferred_element_type=f32)
        up = jnp.dot(select, su_ref[0, rows, :], preferred_element_type=f32)
        sig = jax.nn.sigmoid(gate)
        silu = gate * sig
        act_t[:, rows] = (silu * up * weights).T.astype(bf16)
        f_gate[i] = weights * up * sig * (1.0 + gate * (1.0 - sig))
        f_up[i] = weights * silu
        ag_xy(4, i, ex_x, col_b, x_dev).wait_recv()
        ag_xy(5, i, ex_y, col_a, y_dev).wait_recv()
        ag_xy(6, i, ex_d, col_a, y_dev).wait_recv()
        ag_xy(7, i, ex_d, col_b, x_dev).wait_recv()
        ag_sib(i, False).start()

    def compute(i):
        q = group_at(i)

        @pl.when(i == 0)
        def _():
            for load in loads[2:]:
                load.wait()

        ag_sib(i, True).wait_recv()
        rows = pl.ds(pl.multiple_of(q * rows_g, rows_g), rows_g)
        d_act = lax.dot_general(
            cot_all[rows, :], wd_ref[0], NT, preferred_element_type=f32
        )
        d_gate = (d_act * f_gate[i]).astype(bf16)
        d_up = (d_act * f_up[i]).astype(bf16)

        def partial_of(col):
            wide = pl.ds(col, half)
            value = lax.dot_general(d_gate, wg_ref[0, wide, :], NT, preferred_element_type=f32)
            return value + lax.dot_general(
                d_up, wu_ref[0, wide, :], NT, preferred_element_type=f32
            )

        sib_send[i] = partial_of(sib_col).astype(bf16)
        rs_sib(i).start()
        own_buf[i] = partial_of(my_col)

    def rs_first(i):
        rs_sib(i).wait_recv()
        total = own_buf[i] + sib_recv[i].astype(f32)
        p_buf[i] = total.astype(bf16).reshape(2, 2, tok, half)
        rs_a1(i).start()
        rs_b1(i).start()

    def rs_second(i):
        rs_a1(i).wait_recv()
        left = p_buf[i, y, :, :, pl.ds(0, quarter)].astype(f32) + ra[i].astype(f32)
        a2[i] = left.astype(bf16)
        rs_a2(i).start()
        rs_b1(i).wait_recv()
        right = p_buf[i, :, x, :, pl.ds(quarter, quarter)].astype(f32) + rb[i].astype(f32)
        b2[i] = right.astype(bf16)
        rs_b2(i).start()

    def rs_third(i):
        rs_a2(i).wait_recv()
        rs_b2(i).wait_recv()
        left = a2[i, x].astype(f32) + ra2[i].astype(f32)
        right = b2[i, y].astype(f32) + rb2[i].astype(f32)
        z_send[i] = jnp.concatenate([left, right], axis=1).astype(bf16)

        @pl.when(i > 0)
        def _():
            rs_z(i).start()

    def grad_chunk(j):
        base = jnp.where(j < 2, 1 - r, r) * half + (j % 2) * quarter
        cols = pl.ds(pl.multiple_of(base, quarter), quarter)
        value = jnp.dot(act_t[...], cot_all[:, cols], preferred_element_type=f32)
        land = pl.ds(pl.multiple_of((j % 2) * quarter, quarter), quarter)

        @pl.when(j < 2)
        def _():
            gt_send[:, land] = value.astype(bf16)

        @pl.when(j >= 2)
        def _():
            gd_ref[:, land] = value

        @pl.when(j == 1)
        def _():
            grad_copy.start()

    stages = (ag_first, ag_second, ag_third, compute, rs_first, rs_second, rs_third)
    order = (0, 1, 4, 5, 6, 2, 3)
    last = n_group + len(stages) - 1

    def step(s, carry):
        for lag in order:

            @pl.when((s >= lag) & (s < lag + n_group))
            def _(lag=lag):
                stages[lag](s - lag)

        @pl.when(s >= last - 4)
        def _():
            grad_chunk(s - (last - 4))

        return carry

    lax.fori_loop(0, last, step, 0)

    grad_copy.wait_recv()
    total = z_send[0].astype(f32)
    for i in range(1, n_group):
        rs_z(i).wait_recv()
        total = total + z_recv[i].astype(f32)
    out_ref[...] = total.astype(bf16)

    grad_copy.wait_send()

    def drain(i, carry):
        @pl.when(i > 0)
        def _():
            ag_z(i, False).wait_send()
            ag_mz(i, False).wait_send()
            rs_z(i).wait_send()

        ag_meta(8, i, ex, x_dev).wait_send()
        ag_meta(9, i, ex, y_dev).wait_send()
        ag_meta(10, i, ex, d_dev).wait_send()
        ag_xy(2, i, ex, col_a, x_dev).wait_send()
        ag_xy(3, i, ex, col_b, y_dev).wait_send()
        ag_xy(4, i, ex, col_b, x_dev).wait_send()
        ag_xy(5, i, ex, col_a, y_dev).wait_send()
        ag_xy(6, i, ex_x, col_a, y_dev).wait_send()
        ag_xy(7, i, ex_y, col_b, x_dev).wait_send()
        ag_sib(i, False).wait_send()
        rs_sib(i).wait_send()
        rs_a1(i).wait_send()
        rs_b1(i).wait_send()
        rs_a2(i).wait_send()
        rs_b2(i).wait_send()
        return carry

    lax.fori_loop(0, n_group, drain, 0)


def finish_kernel(rows_ref, own_ref, other_ref, out_ref, gd_ref):
    out_ref[...] = rows_ref[...]
    gd_ref[0] = own_ref[...] + other_ref[...].astype(jnp.float32)


def dense_plan(cotangent, expert_ids, gate_probs, saved_gate, saved_up, w_gate, w_up, w_down):
    n_group = lax.axis_size("group")
    n_expert = lax.axis_size("expert")
    tok, width = cotangent.shape
    half, quarter = width // 2, width // 4
    hidden = w_down.shape[1]
    experts = n_group * n_expert // 2
    blocks = n_group * n_expert
    rows_g = n_expert * tok
    bf16, f32 = jnp.bfloat16, jnp.float32
    vmem = pl.BlockSpec(memory_space=pltpu.VMEM)
    kinds = 18
    cotangent, saved_gate, saved_up, w_gate, w_up, w_down = (
        pltpu.with_memory_space_constraint(value, pltpu.HBM)
        for value in (cotangent, saved_gate, saved_up, w_gate, w_up, w_down)
    )
    here = pl.BlockSpec(memory_space=pltpu.HBM)
    rows, own, other = pl.pallas_call(
        functools.partial(dense_kernel, n_group, n_expert),
        out_shape=(
            jax.ShapeDtypeStruct((tok, half), bf16),
            jax.ShapeDtypeStruct((hidden, half), f32),
            jax.ShapeDtypeStruct((hidden, half), bf16),
        ),
        in_specs=[here, vmem, vmem] + [here] * 5,
        out_specs=(vmem, vmem, vmem),
        scratch_shapes=[
            pltpu.VMEM(saved_gate.shape, bf16),
            pltpu.VMEM(saved_up.shape, bf16),
            pltpu.VMEM(w_gate.shape, bf16),
            pltpu.VMEM(w_up.shape, bf16),
            pltpu.VMEM(w_down.shape, bf16),
            pltpu.VMEM((blocks * tok, width), bf16),
            pltpu.VMEM((blocks, experts, 2 * tok), f32),
            pltpu.VMEM((hidden, blocks * tok), bf16),
            pltpu.VMEM((n_group, rows_g, hidden), f32),
            pltpu.VMEM((n_group, rows_g, hidden), f32),
            pltpu.VMEM((n_group, rows_g, half), f32),
            pltpu.VMEM((n_group, rows_g, half), bf16),
            pltpu.VMEM((n_group, rows_g, half), bf16),
            pltpu.VMEM((n_group, 2, 2, tok, half), bf16),
            pltpu.VMEM((n_group, 2, tok, quarter), bf16),
            pltpu.VMEM((n_group, 2, tok, quarter), bf16),
            pltpu.VMEM((n_group, 2, tok, quarter), bf16),
            pltpu.VMEM((n_group, 2, tok, quarter), bf16),
            pltpu.VMEM((n_group, tok, quarter), bf16),
            pltpu.VMEM((n_group, tok, quarter), bf16),
            pltpu.VMEM((n_group, tok, half), bf16),
            pltpu.VMEM((n_group, tok, half), bf16),
            pltpu.VMEM((hidden, half), bf16),
            pltpu.SemaphoreType.DMA((kinds, n_group)),
            pltpu.SemaphoreType.DMA((kinds, n_group)),
            pltpu.SemaphoreType.DMA((2,)),
            pltpu.SemaphoreType.DMA((6,)),
        ],
        compiler_params=pltpu.CompilerParams(
            collective_id=0, has_side_effects=True, vmem_limit_bytes=40 * 1024 * 1024
        ),
    )(
        cotangent,
        expert_ids[0].T,
        gate_probs[0].T,
        saved_gate,
        saved_up,
        w_gate,
        w_up,
        w_down,
    )
    return pl.pallas_call(
        finish_kernel,
        out_shape=(
            jax.ShapeDtypeStruct((tok, half), bf16),
            jax.ShapeDtypeStruct((1, hidden, half), f32),
        ),
        in_specs=[vmem] * 3,
        out_specs=(vmem, vmem),
        compiler_params=pltpu.CompilerParams(vmem_limit_bytes=8 * 1024 * 1024),
    )(rows, own, other)


def on_device(cotangent, expert_ids, gate_probs, saved_gate, saved_up, w_gate, w_up, w_down):
    n_group = lax.axis_size("group")
    n_expert = lax.axis_size("expert")
    n_replica = lax.axis_size("replica")
    tok_rows = cotangent.shape[0]
    capacity = saved_gate.shape[1] // (n_group * n_expert)
    small = n_group == 4 and n_expert == 4 and n_replica == 2
    plan = routed_plan
    if small and capacity == tok_rows and 2 * tok_rows == 128:
        plan = dense_plan
    return plan(cotangent, expert_ids, gate_probs, saved_gate, saved_up, w_gate, w_up, w_down)


def solution(mesh):
    return jax.shard_map(
        on_device,
        mesh=mesh,
        in_specs=(
            P(("group", "expert"), None),
            P("replica", ("group", "expert"), None),
            P("replica", ("group", "expert"), None),
            P(("group", "expert"), "replica", None),
            P(("group", "expert"), "replica", None),
            P(("group", "expert"), None, None),
            P(("group", "expert"), None, None),
            P(("group", "expert"), None, None),
        ),
        out_specs=(P(("group", "expert"), "replica"), P(("group", "expert"), None, "replica")),
        check_vma=False,
    )
```

```python
import functools

import jax
import jax.numpy as jnp
from jax import lax
from jax.experimental import pallas as pl
from jax.experimental.pallas import tpu as pltpu
from jax.sharding import PartitionSpec as P

MESH = pl.DeviceIdType.MESH
NT = (((1,), (1,)), ((), ()))


def from_partner(value, axis, bit):
    mask = 2**bit
    pairs = [(source, source ^ mask) for source in range(lax.axis_size(axis))]
    return lax.ppermute(value, axis, pairs)


def routed_plan(cotangent, expert_ids, gate_probs, saved_gate, saved_up, w_gate, w_up, w_down):
    n_group = lax.axis_size("group")
    n_expert = lax.axis_size("expert")
    tok_rows, model_width = cotangent.shape
    pick_count = expert_ids.shape[2]
    experts = n_group * n_expert // 2
    half_width = model_width // 2
    capacity = saved_gate.shape[1] // (n_group * n_expert)
    assigned = tok_rows * pick_count
    flat_ids = expert_ids.reshape(assigned)
    positions = jnp.arange(assigned, dtype=jnp.int32)
    same_expert = (flat_ids[:, None] == flat_ids[None, :]) & (
        positions[None, :] < positions[:, None]
    )
    slot_pos = jnp.sum(same_expert.astype(jnp.int32), axis=1)
    target = flat_ids * capacity + slot_pos
    places = jnp.arange(experts * capacity, dtype=jnp.int32)
    dispatch_map = (places[:, None] == target[None, :]).astype(jnp.bfloat16)
    scaled = (gate_probs[0][:, :, None] * cotangent[:, None, :].astype(jnp.float32)).astype(
        jnp.bfloat16
    )
    scaled = scaled.reshape(assigned, model_width)
    packed = jnp.dot(dispatch_map, scaled, preferred_element_type=jnp.float32).astype(jnp.bfloat16)
    packed = packed.reshape(n_group // 2, n_expert, capacity, 2, half_width)
    packed = packed.transpose(0, 3, 1, 2, 4).reshape(n_group, n_expert, capacity, half_width)
    arrived = lax.all_to_all(
        lax.all_to_all(packed, "expert", split_axis=1, concat_axis=1, tiled=True),
        "group",
        split_axis=0,
        concat_axis=0,
        tiled=True,
    )
    partner = from_partner(arrived, "group", 0)
    low_half = lax.axis_index("group") % 2 == 0
    front_half = jnp.where(low_half, arrived, partner)
    back_half = jnp.where(low_half, partner, arrived)
    dy_slots = jnp.concatenate([front_half, back_half], axis=3).reshape(-1, model_width)
    pre_gate = saved_gate[0].astype(jnp.float32)
    pre_up = saved_up[0].astype(jnp.float32)
    sigmoid_gate = jax.nn.sigmoid(pre_gate)
    silu_gate = pre_gate * sigmoid_gate
    activation = (silu_gate * pre_up).astype(jnp.bfloat16)
    d_act = lax.dot_general(
        dy_slots, w_down[0], (((1,), (1,)), ((), ())), preferred_element_type=jnp.float32
    )
    d_gate = (d_act * pre_up * sigmoid_gate * (1.0 + pre_gate * (1.0 - sigmoid_gate))).astype(
        jnp.bfloat16
    )
    d_up = (d_act * silu_gate).astype(jnp.bfloat16)
    partial_value = lax.dot_general(
        d_gate, w_gate[0], (((1,), (1,)), ((), ())), preferred_element_type=jnp.float32
    )
    partial_value = partial_value + lax.dot_general(
        d_up, w_up[0], (((1,), (1,)), ((), ())), preferred_element_type=jnp.float32
    )
    partial_value = partial_value.astype(jnp.bfloat16)
    own_half = jnp.where(low_half, partial_value[:, :half_width], partial_value[:, half_width:])
    peer_half = jnp.where(low_half, partial_value[:, half_width:], partial_value[:, :half_width])
    received = from_partner(peer_half, "group", 0)
    combined = (own_half.astype(jnp.float32) + received.astype(jnp.float32)).astype(jnp.bfloat16)
    combined = combined.reshape(n_group, n_expert, capacity, half_width)
    grad_terms = lax.dot_general(
        activation, dy_slots, (((0,), (0,)), ((), ())), preferred_element_type=jnp.float32
    )
    returned = lax.all_to_all(
        lax.all_to_all(combined, "group", split_axis=0, concat_axis=0, tiled=True),
        "expert",
        split_axis=1,
        concat_axis=1,
        tiled=True,
    )
    home_rows = returned.reshape(n_group // 2, 2, n_expert, capacity, half_width)
    home_rows = home_rows.transpose(0, 2, 3, 1, 4).reshape(experts * capacity, model_width)
    per_assign = lax.dot_general(
        dispatch_map, home_rows, (((0,), (0,)), ((), ())), preferred_element_type=jnp.float32
    )
    home_sum = jnp.sum(per_assign.reshape(tok_rows, pick_count, model_width), axis=1)
    grad_down, grad_input = (
        lax.psum_scatter(grad_terms, "replica", scatter_dimension=1, tiled=True),
        lax.psum_scatter(home_sum, "replica", scatter_dimension=1, tiled=True),
    )
    return (grad_input.astype(jnp.bfloat16), grad_down[None])


def dense_kernel(
    n_group,
    n_expert,
    cot_ref,
    ids_ref,
    prob_ref,
    sg_hbm,
    su_hbm,
    wg_hbm,
    wu_hbm,
    wd_hbm,
    out_ref,
    gd_ref,
    gt_recv,
    sg_ref,
    su_ref,
    wg_ref,
    wu_ref,
    wd_ref,
    cot_all,
    meta_all,
    act_t,
    f_gate,
    f_up,
    own_buf,
    sib_send,
    sib_recv,
    p_buf,
    ra,
    rb,
    a2,
    b2,
    ra2,
    rb2,
    z_send,
    z_recv,
    gt_send,
    ssem,
    rsem,
    gsem,
    lsem,
):
    tok, width = cot_ref.shape
    half = width // 2
    quarter = half // 2
    rows_g = n_expert * tok
    picks = ids_ref.shape[0]
    experts = meta_all.shape[1]
    f32, bf16 = jnp.float32, jnp.bfloat16
    g = lax.axis_index("group")
    ex = lax.axis_index("expert")
    r = lax.axis_index("replica")
    x, y = ex % 2, ex // 2
    nx, ny = 1 - x, 1 - y
    ex_x, ex_y, ex_d = y * 2 + nx, ny * 2 + x, ny * 2 + nx
    x_dev, y_dev, d_dev = (g, ex_x, r), (g, ex_y, r), (g, ex_d, r)
    sib_dev = (g, ex, 1 - r)

    def group_at(i):
        low = (g % 2 + i % 2) % 2
        high = (g // 2 + i // 2) % 2
        return low + 2 * high

    my_col = pl.multiple_of(r * half, half)
    sib_col = pl.multiple_of((1 - r) * half, half)
    col_a = my_col
    col_b = pl.multiple_of(r * half + quarter, quarter)

    def row_of(q, e):
        return pl.multiple_of((q * n_expert + e) * tok, tok)

    def rcopy(kind, i, src, dst, dev):
        return pltpu.make_async_remote_copy(
            src_ref=src,
            dst_ref=dst,
            send_sem=ssem.at[kind, i],
            recv_sem=rsem.at[kind, i],
            device_id=dev,
            device_id_type=MESH,
        )

    def block(q, e, col, size):
        return cot_all.at[pl.ds(row_of(q, e), tok), pl.ds(col, size)]

    def z_dev(i):
        return (group_at(i), ex, r)

    def ag_z(i, recv):
        land = block(group_at(i), ex, my_col, half) if recv else block(g, ex, my_col, half)
        return rcopy(0, i, land, land, z_dev(i))

    def ag_mz(i, recv):
        ref = meta_all.at[(group_at(i) if recv else g) * n_expert + ex]
        return rcopy(1, i, ref, ref, z_dev(i))

    def ag_xy(kind, i, e, col, dev):
        ref = block(group_at(i), e, col, quarter)
        return rcopy(kind, i, ref, ref, dev)

    def ag_meta(kind, i, e, dev):
        ref = meta_all.at[group_at(i) * n_expert + e]
        return rcopy(kind, i, ref, ref, dev)

    def ag_sib(i, recv):
        rows = pl.ds(row_of(group_at(i), 0), rows_g)
        ref = cot_all.at[rows, pl.ds(sib_col if recv else my_col, half)]
        return rcopy(11, i, ref, ref, sib_dev)

    def rs_sib(i):
        return rcopy(12, i, sib_send.at[i], sib_recv.at[i], sib_dev)

    def rs_a1(i):
        return rcopy(13, i, p_buf.at[i, ny, :, :, pl.ds(0, quarter)], ra.at[i], y_dev)

    def rs_b1(i):
        return rcopy(14, i, p_buf.at[i, :, nx, :, pl.ds(quarter, quarter)], rb.at[i], x_dev)

    def rs_a2(i):
        return rcopy(15, i, a2.at[i, nx], ra2.at[i], x_dev)

    def rs_b2(i):
        return rcopy(16, i, b2.at[i, ny], rb2.at[i], y_dev)

    def rs_z(i):
        return rcopy(17, i, z_send.at[i], z_recv.at[i], z_dev(i))

    grad_copy = pltpu.make_async_remote_copy(
        src_ref=gt_send,
        dst_ref=gt_recv,
        send_sem=gsem.at[0],
        recv_sem=gsem.at[1],
        device_id=sib_dev,
        device_id_type=MESH,
    )

    barrier = pltpu.get_barrier_semaphore()
    peers = [z_dev(i) for i in range(1, n_group)] + [x_dev, y_dev, d_dev, sib_dev]
    for dev in peers:
        pl.semaphore_signal(barrier, inc=1, device_id=dev, device_id_type=MESH)

    place = pltpu.make_async_copy(
        cot_ref.at[:, pl.ds(my_col, half)], block(g, ex, my_col, half), lsem.at[0]
    )
    place.start()
    loads = [
        pltpu.make_async_copy(src, dst, lsem.at[1 + k])
        for k, (src, dst) in enumerate(
            [
                (sg_hbm, sg_ref),
                (su_hbm, su_ref),
                (wd_hbm, wd_ref),
                (wg_hbm, wg_ref),
                (wu_hbm, wu_ref),
            ]
        )
    ]
    for load in loads:
        load.start()
    named_by = lax.broadcasted_iota(jnp.int32, (experts, tok), 0)
    named = jnp.zeros((experts, tok), f32)
    weight = jnp.zeros((experts, tok), f32)
    for k in range(picks):
        same = ids_ref[k : k + 1, :] == named_by
        named = named + jnp.where(same, 1.0, 0.0)
        weight = weight + jnp.where(same, prob_ref[k : k + 1, :], 0.0)
    before = lax.broadcasted_iota(jnp.int32, (tok, tok), 0) < lax.broadcasted_iota(
        jnp.int32, (tok, tok), 1
    )
    slot = jnp.dot(
        named.astype(bf16), jnp.where(before, 1.0, 0.0).astype(bf16), preferred_element_type=f32
    )
    slot = jnp.where(named > 0.5, slot, -1.0)
    meta_all[g * n_expert + ex] = jnp.concatenate([slot, weight], axis=1)
    place.wait()
    pl.semaphore_wait(barrier, len(peers))

    for i in range(1, n_group):
        ag_mz(i, False).start()
    for i in range(1, n_group):
        ag_z(i, False).start()

    expert = (g // 2) * n_expert + ex
    eye = lax.broadcasted_iota(jnp.int32, (2 * tok, 2 * tok), 0) == lax.broadcasted_iota(
        jnp.int32, (2 * tok, 2 * tok), 1
    )
    place_lane = lax.broadcasted_iota(jnp.int32, (tok, rows_g), 1).astype(f32)

    def ag_first(i):
        @pl.when(i > 0)
        def _():
            ag_mz(i, True).wait_recv()
            ag_z(i, True).wait_recv()

        ag_meta(8, i, ex, x_dev).start()
        ag_meta(9, i, ex, y_dev).start()
        ag_meta(10, i, ex, d_dev).start()
        ag_xy(2, i, ex, col_a, x_dev).start()
        ag_xy(3, i, ex, col_b, y_dev).start()
        ag_xy(4, i, ex, col_b, x_dev).start()
        ag_xy(5, i, ex, col_a, y_dev).start()

    def ag_second(i):
        ag_xy(2, i, ex_x, col_a, x_dev).wait_recv()
        ag_xy(6, i, ex_x, col_a, y_dev).start()
        ag_xy(3, i, ex_y, col_b, y_dev).wait_recv()
        ag_xy(7, i, ex_y, col_b, x_dev).start()

    def ag_third(i):
        q = group_at(i)
        ag_meta(8, i, ex_x, x_dev).wait_recv()
        ag_meta(9, i, ex_y, y_dev).wait_recv()
        ag_meta(10, i, ex_d, d_dev).wait_recv()
        picked, weights = [], []
        for b in range(n_expert):
            row = meta_all[q * n_expert + b, pl.ds(expert, 1), :]
            col = jnp.sum(jnp.where(eye, row, 0.0), axis=1, keepdims=True)
            slot_col = col[:tok]
            target = jnp.where(slot_col < -0.5, -1.0, slot_col + float(b * tok))
            picked.append(jnp.where(place_lane == target, 1.0, 0.0))
            weights.append(col[tok:])
        select = jnp.concatenate(picked, axis=0).astype(bf16)
        weights = jnp.concatenate(weights, axis=0)
        rows = pl.ds(pl.multiple_of(q * rows_g, rows_g), rows_g)

        @pl.when(i == 0)
        def _():
            for load in loads[:2]:
                load.wait()

        gate = jnp.dot(select, sg_ref[0, rows, :], preferred_element_type=f32)
        up = jnp.dot(select, su_ref[0, rows, :], preferred_element_type=f32)
        sig = jax.nn.sigmoid(gate)
        silu = gate * sig
        act_t[:, rows] = (silu * up * weights).T.astype(bf16)
        f_gate[i] = weights * up * sig * (1.0 + gate * (1.0 - sig))
        f_up[i] = weights * silu
        ag_xy(4, i, ex_x, col_b, x_dev).wait_recv()
        ag_xy(5, i, ex_y, col_a, y_dev).wait_recv()
        ag_xy(6, i, ex_d, col_a, y_dev).wait_recv()
        ag_xy(7, i, ex_d, col_b, x_dev).wait_recv()
        ag_sib(i, False).start()

    def compute(i):
        q = group_at(i)

        @pl.when(i == 1)
        def _():
            for load in loads[2:]:
                load.wait()

        ag_sib(i, True).wait_recv()
        rows = pl.ds(pl.multiple_of(q * rows_g, rows_g), rows_g)
        d_act = lax.dot_general(
            cot_all[rows, :], wd_ref[0], NT, preferred_element_type=f32
        )
        d_gate = (d_act * f_gate[i]).astype(bf16)
        d_up = (d_act * f_up[i]).astype(bf16)

        def partial_of(col):
            wide = pl.ds(col, half)
            value = lax.dot_general(d_gate, wg_ref[0, wide, :], NT, preferred_element_type=f32)
            return value + lax.dot_general(
                d_up, wu_ref[0, wide, :], NT, preferred_element_type=f32
            )

        sib_send[i] = partial_of(sib_col).astype(bf16)
        rs_sib(i).start()
        own_buf[i] = partial_of(my_col)

    def rs_first(i):
        rs_sib(i).wait_recv()
        total = own_buf[i] + sib_recv[i].astype(f32)
        p_buf[i] = total.astype(bf16).reshape(2, 2, tok, half)
        rs_a1(i).start()
        rs_b1(i).start()

    def rs_second(i):
        rs_a1(i).wait_recv()
        left = p_buf[i, y, :, :, pl.ds(0, quarter)].astype(f32) + ra[i].astype(f32)
        a2[i] = left.astype(bf16)
        rs_a2(i).start()
        rs_b1(i).wait_recv()
        right = p_buf[i, :, x, :, pl.ds(quarter, quarter)].astype(f32) + rb[i].astype(f32)
        b2[i] = right.astype(bf16)
        rs_b2(i).start()

    def rs_third(i):
        rs_a2(i).wait_recv()
        rs_b2(i).wait_recv()
        left = a2[i, x].astype(f32) + ra2[i].astype(f32)
        right = b2[i, y].astype(f32) + rb2[i].astype(f32)
        z_send[i] = jnp.concatenate([left, right], axis=1).astype(bf16)

        @pl.when(i > 0)
        def _():
            rs_z(i).start()

    def grad_chunk(j):
        base = jnp.where(j < 2, 1 - r, r) * half + (j % 2) * quarter
        cols = pl.ds(pl.multiple_of(base, quarter), quarter)
        value = jnp.dot(act_t[...], cot_all[:, cols], preferred_element_type=f32)
        land = pl.ds(pl.multiple_of((j % 2) * quarter, quarter), quarter)

        @pl.when(j < 2)
        def _():
            gt_send[:, land] = value.astype(bf16)

        @pl.when(j >= 2)
        def _():
            gd_ref[:, land] = value

        @pl.when(j == 1)
        def _():
            grad_copy.start()

    stages = (ag_first, ag_second, ag_third, compute, rs_first, rs_second, rs_third)
    order = (0, 1, 4, 5, 6, 2, 3)
    lags = (0, 1, 2, 4, 5, 6, 7)
    last = n_group + lags[-1]

    def step(s, carry):
        for k in order:

            @pl.when((s >= lags[k]) & (s < lags[k] + n_group))
            def _(k=k):
                stages[k](s - lags[k] if k < 3 else (s - lags[k] + 1) % n_group)

        @pl.when(s >= last - 4)
        def _():
            grad_chunk(s - (last - 4))

        return carry

    lax.fori_loop(0, last, step, 0)

    grad_copy.wait_recv()
    total = z_send[0].astype(f32)
    for i in range(1, n_group):
        rs_z(i).wait_recv()
        total = total + z_recv[i].astype(f32)
    out_ref[...] = total.astype(bf16)

    grad_copy.wait_send()

    def drain(i, carry):
        @pl.when(i > 0)
        def _():
            ag_z(i, False).wait_send()
            ag_mz(i, False).wait_send()
            rs_z(i).wait_send()

        ag_meta(8, i, ex, x_dev).wait_send()
        ag_meta(9, i, ex, y_dev).wait_send()
        ag_meta(10, i, ex, d_dev).wait_send()
        ag_xy(2, i, ex, col_a, x_dev).wait_send()
        ag_xy(3, i, ex, col_b, y_dev).wait_send()
        ag_xy(4, i, ex, col_b, x_dev).wait_send()
        ag_xy(5, i, ex, col_a, y_dev).wait_send()
        ag_xy(6, i, ex_x, col_a, y_dev).wait_send()
        ag_xy(7, i, ex_y, col_b, x_dev).wait_send()
        ag_sib(i, False).wait_send()
        rs_sib(i).wait_send()
        rs_a1(i).wait_send()
        rs_b1(i).wait_send()
        rs_a2(i).wait_send()
        rs_b2(i).wait_send()
        return carry

    lax.fori_loop(0, n_group, drain, 0)


def finish_kernel(rows_ref, own_ref, other_ref, out_ref, gd_ref):
    out_ref[...] = rows_ref[...]
    gd_ref[0] = own_ref[...] + other_ref[...].astype(jnp.float32)


def dense_plan(cotangent, expert_ids, gate_probs, saved_gate, saved_up, w_gate, w_up, w_down):
    n_group = lax.axis_size("group")
    n_expert = lax.axis_size("expert")
    tok, width = cotangent.shape
    half, quarter = width // 2, width // 4
    hidden = w_down.shape[1]
    experts = n_group * n_expert // 2
    blocks = n_group * n_expert
    rows_g = n_expert * tok
    bf16, f32 = jnp.bfloat16, jnp.float32
    vmem = pl.BlockSpec(memory_space=pltpu.VMEM)
    kinds = 18
    cotangent, saved_gate, saved_up, w_gate, w_up, w_down = (
        pltpu.with_memory_space_constraint(value, pltpu.HBM)
        for value in (cotangent, saved_gate, saved_up, w_gate, w_up, w_down)
    )
    ids, probs = (
        pltpu.with_memory_space_constraint(value[0].T, pltpu.HBM)
        for value in (expert_ids, gate_probs)
    )
    here = pl.BlockSpec(memory_space=pltpu.HBM)
    rows, own, other = pl.pallas_call(
        functools.partial(dense_kernel, n_group, n_expert),
        out_shape=(
            jax.ShapeDtypeStruct((tok, half), bf16),
            jax.ShapeDtypeStruct((hidden, half), f32),
            jax.ShapeDtypeStruct((hidden, half), bf16),
        ),
        in_specs=[here, vmem, vmem] + [here] * 5,
        out_specs=(vmem, vmem, vmem),
        scratch_shapes=[
            pltpu.VMEM(saved_gate.shape, bf16),
            pltpu.VMEM(saved_up.shape, bf16),
            pltpu.VMEM(w_gate.shape, bf16),
            pltpu.VMEM(w_up.shape, bf16),
            pltpu.VMEM(w_down.shape, bf16),
            pltpu.VMEM((blocks * tok, width), bf16),
            pltpu.VMEM((blocks, experts, 2 * tok), f32),
            pltpu.VMEM((hidden, blocks * tok), bf16),
            pltpu.VMEM((n_group, rows_g, hidden), f32),
            pltpu.VMEM((n_group, rows_g, hidden), f32),
            pltpu.VMEM((n_group, rows_g, half), f32),
            pltpu.VMEM((n_group, rows_g, half), bf16),
            pltpu.VMEM((n_group, rows_g, half), bf16),
            pltpu.VMEM((n_group, 2, 2, tok, half), bf16),
            pltpu.VMEM((n_group, 2, tok, quarter), bf16),
            pltpu.VMEM((n_group, 2, tok, quarter), bf16),
            pltpu.VMEM((n_group, 2, tok, quarter), bf16),
            pltpu.VMEM((n_group, 2, tok, quarter), bf16),
            pltpu.VMEM((n_group, tok, quarter), bf16),
            pltpu.VMEM((n_group, tok, quarter), bf16),
            pltpu.VMEM((n_group, tok, half), bf16),
            pltpu.VMEM((n_group, tok, half), bf16),
            pltpu.VMEM((hidden, half), bf16),
            pltpu.SemaphoreType.DMA((kinds, n_group)),
            pltpu.SemaphoreType.DMA((kinds, n_group)),
            pltpu.SemaphoreType.DMA((2,)),
            pltpu.SemaphoreType.DMA((6,)),
        ],
        compiler_params=pltpu.CompilerParams(
            collective_id=0, has_side_effects=True, vmem_limit_bytes=40 * 1024 * 1024
        ),
    )(
        cotangent,
        ids,
        probs,
        saved_gate,
        saved_up,
        w_gate,
        w_up,
        w_down,
    )
    return pl.pallas_call(
        finish_kernel,
        out_shape=(
            jax.ShapeDtypeStruct((tok, half), bf16),
            jax.ShapeDtypeStruct((1, hidden, half), f32),
        ),
        in_specs=[vmem] * 3,
        out_specs=(vmem, vmem),
        compiler_params=pltpu.CompilerParams(vmem_limit_bytes=8 * 1024 * 1024),
    )(rows, own, other)


def on_device(cotangent, expert_ids, gate_probs, saved_gate, saved_up, w_gate, w_up, w_down):
    n_group = lax.axis_size("group")
    n_expert = lax.axis_size("expert")
    n_replica = lax.axis_size("replica")
    tok_rows = cotangent.shape[0]
    capacity = saved_gate.shape[1] // (n_group * n_expert)
    small = n_group == 4 and n_expert == 4 and n_replica == 2
    plan = routed_plan
    if small and capacity == tok_rows and 2 * tok_rows == 128:
        plan = dense_plan
    return plan(cotangent, expert_ids, gate_probs, saved_gate, saved_up, w_gate, w_up, w_down)


def solution(mesh):
    return jax.shard_map(
        on_device,
        mesh=mesh,
        in_specs=(
            P(("group", "expert"), None),
            P("replica", ("group", "expert"), None),
            P("replica", ("group", "expert"), None),
            P(("group", "expert"), "replica", None),
            P(("group", "expert"), "replica", None),
            P(("group", "expert"), None, None),
            P(("group", "expert"), None, None),
            P(("group", "expert"), None, None),
        ),
        out_specs=(P(("group", "expert"), "replica"), P(("group", "expert"), None, "replica")),
        check_vma=False,
    )
```
